256 devices in a mesh: tok: 8 (over z), tp: 16 (over y, x), grp: 2 (over core).
Axes of the slice: x: 4, y: 4, z: 8, core: 2. Of those that a mesh axis runs over, the one named last changes fastest.
Arguments:
- hidden: bfloat16 [2048, 6144], P(('tok', 'grp'), 'tp'), may hold values from -6 to 6
- gain: bfloat16 [6144], P('tp'), may hold values from 0.5 to 1.5
- expert_ids: int32 [2048, 2], P(('tok', 'grp')), may hold values from 0 to 7, all different within a row; in each aligned block of 128 rows (0 to 127, 128 to 255, ...) at most 40 rows name the same one
- gate_weights: float32 [2048, 2], P(('tok', 'grp')), may hold values from 0.1 to 0.9
- segment_ids: int32 [2048], P(('tok', 'grp')), may hold values from 0 to 15, never falling along the last dimension, each value on 1 to 384 neighbouring positions
- upstream: bfloat16 [2048, 6144], P(('tok', 'grp'), 'tp'), may hold values from -6 to 6
- w_gate: bfloat16 [8, 6144, 8192], P('tok', None, ('tp', 'grp')), may hold values from -0.078125 to 0.078125
- w_up: bfloat16 [8, 6144, 8192], P('tok', None, ('tp', 'grp')), may hold values from -0.078125 to 0.078125
- w_down: bfloat16 [8, 8192, 6144], P('tok', ('tp', 'grp')), may hold values from -0.0625 to 0.0625
Outputs:
- mixed: bfloat16 [2048, 6144], P(('tok', 'grp'), 'tp')
- importance: float32 [8, 8192], P('tok', ('tp', 'grp'))
The draws below stay inside these ranges and needn't reach their ends.
Inputs may be any that keep to these rules, and one draw needn't show every extreme that they name: `expert_ids`: each token names 2 different experts. Within the tokens of one token shard (aligned blocks of 128 rows) no expert is named by more than 40 tokens, and in some block one expert is named by exactly 40. `segment_ids`: never falling along the tokens; every document holds between 1 and 384 tokens.
All inputs are finite; a program needn't handle non-finite values.
Results may differ from the reference program's by a relative error of at most 0.0095.
Values may be sent and summed in bfloat16 or wider, within the bound.
No kernel may reach another device: no remote copies, remote signals or barrier semaphores. Data moves between devices by JAX's collectives and lax.ppermute only.
A program may use at most 128 MiB of HBM per device.

```python
import math
import jax
import jax.numpy as jnp
import numpy as np
from jax import lax

D = 6144
TOP = 2
FW = 8192
RTOK = 128
EXPERTS = 8
CAP = 40
ROWS = 640
NDOCS = 16
TOKENS = 2048
N_TOK = 8
N_TP = 16
N_GRP = 2


def level_of(key, dims, pieces, least, high):
    factor_of = 1.0
    for dim, shards_of in pieces:
        draws = jax.random.uniform(jax.random.fold_in(jax.random.fold_in(key, 6), dim), (shards_of,), jnp.float32, least / len(pieces), high / len(pieces))
        factor_of = factor_of * jnp.repeat(jnp.exp(draws), dims[dim] // shards_of).reshape((-1,) + (1,) * (len(dims) - 1 - dim))
    return factor_of


def length_profile(amount, total, limit, lean):
    loads = [(1 << 20) // math.isqrt(standing ** lean) + 1 for standing in range(2, amount + 1)]
    spare, given = total - limit - (amount - 1), [1] * (amount - 1)
    while spare > 0:
        candidates = [i for i in range(amount - 1) if given[i] < limit]
        pool, budget = sum([loads[i] for i in candidates]), spare
        for i in candidates:
            extra = min(limit - given[i], max(1, budget * loads[i] // pool), spare)
            given[i] = given[i] + extra
            spare = spare - extra
    return np.array([limit] + given)


def uneven(own_key, number_of, total, bound, lean):
    if number_of == 2:
        one = jax.random.randint(own_key, (), max(1, total - bound), min(bound, total - 1) + 1)
        return jnp.stack([one, total - one])
    sizes = jnp.asarray(length_profile(number_of, total, bound, lean), jnp.int32)
    twos = (number_of - 1) // 2
    source_of, sink = sizes[1:1 + 2 * twos:2], sizes[2:2 + 2 * twos:2]
    room = jnp.minimum(source_of - 1, bound - sink)
    shifted = jax.random.randint(jax.random.fold_in(own_key, 1), (twos,), 0, 1 << 20) % (room + 1)
    sizes = sizes.at[1:1 + 2 * twos:2].set(source_of - shifted).at[2:2 + 2 * twos:2].set(sink + shifted)
    return sizes[jax.random.permutation(jax.random.fold_in(own_key, 2), number_of)]


def routed_block(own_key, own, number, rows, count, top, bound, skew):
    ranking = jax.random.permutation(own_key, count)
    packed, ordinary = portions_of(count, rows * top, bound, skew, True), portions_of(count, rows * top, bound, skew, False)
    places = jnp.arange(count)

    def named(lengths, turn):
        used = int((lengths > 0).sum())
        fixed = max(1, used // 4)
        shifted = fixed + (places - fixed + turn * (used - fixed)) % max(1, count - fixed)
        return jnp.zeros((count,), jnp.int32).at[ranking[jnp.where(places < fixed, places, shifted)]].set(jnp.asarray(lengths, jnp.int32))

    lengths = jnp.where(number % 4 == 0, named(packed, number // 4), named(ordinary, number - number // 4 - 1))
    mixed = jax.random.permutation(jax.random.fold_in(own, 3), count)
    donor, sink = mixed[0:count // 2 * 2:2], mixed[1:count // 2 * 2:2]
    margin = jnp.minimum(lengths[donor] - 1, bound - lengths[sink]) // 2
    margin = jnp.where((donor == ranking[0]) | (sink == ranking[0]) | (lengths[sink] == 0), 0, jnp.maximum(margin, 0))
    shifted = jax.random.randint(jax.random.fold_in(own, 4), (count // 2,), 0, 1 << 20) % (margin + 1)
    lengths = lengths.at[donor].add(-shifted).at[sink].add(shifted)
    items = jnp.searchsorted(jnp.cumsum(lengths), jnp.arange(rows * top), side="right").astype(jnp.int32)
    table = items.reshape(top, rows).T
    table = table[jax.random.permutation(jax.random.fold_in(own, 1), rows)]
    turn = jax.random.randint(jax.random.fold_in(own, 2), (rows, 1), 0, top)
    return jnp.take_along_axis(table, (jnp.arange(top)[None, :] + turn) % top, axis=1)


def portions_of(amount, total, bound, lean, full):
    loads = [(1 << 20) // math.isqrt(grade ** lean) + 1 for grade in range(1, amount + 1)]
    largest = bound if full else min(bound, max(-(-total // amount), total * loads[0] // sum(loads)))
    least = 1 if total - largest >= amount - 1 else 0
    given, rest = [largest] + [least] * (amount - 1), total - largest - least * (amount - 1)
    while rest > 0:
        candidates = [i for i in range(1, amount) if given[i] < largest] or [i for i in range(1, amount) if given[i] < bound]
        whole, left = sum([loads[i] for i in candidates]), rest
        for i in candidates:
            more = min(bound - given[i], max(1, left * loads[i] // whole), rest)
            given[i] = given[i] + more
            rest = rest - more
    return np.array(given)


def noise(rng, shape, width, most, shards=(), kind=jnp.bfloat16):
    drawn = jax.random.normal(rng, shape, jnp.float32) * width
    if len(shards) > 0:
        drawn = level_of(rng, shape, shards, -0.22, 0.18) * drawn
    return jnp.clip(drawn, min=-most, max=most).astype(kind)


def setup_inputs(seed: int = 0) -> dict:
    key_list = jax.random.split(jax.random.key(seed), 10)
    hidden = noise(key_list[0], (TOKENS, D), 1.0, 6.0, ((0, 16), (1, 16)))
    gain = jnp.clip(1.0 + 0.1 * jax.random.normal(key_list[1], (D,), jnp.float32), 0.5, 1.5).astype(jnp.bfloat16)
    expert_ids_keys = jax.random.split(jax.random.fold_in(key_list[2], 1), TOKENS // RTOK)
    expert_ids_turns = jax.random.permutation(jax.random.fold_in(key_list[2], 3), TOKENS // RTOK)
    expert_ids = jax.vmap(lambda own, number: routed_block(jax.random.fold_in(key_list[2], 2), own, number, RTOK, EXPERTS, TOP, CAP, 2))(expert_ids_keys, expert_ids_turns).reshape((TOKENS, TOP))
    gate_weights = jnp.clip(0.1 + 0.79999997 * jax.random.uniform(key_list[3], (TOKENS, TOP), jnp.float32) ** level_of(key_list[3], (TOKENS, TOP), ((0, 16),), -0.2, 0.2), 0.1, 0.9)
    segment_ids = jnp.searchsorted(jnp.cumsum(uneven(key_list[4], NDOCS, TOKENS, 3 * RTOK, 2)), jnp.arange(TOKENS), side="right").astype(jnp.int32)
    upstream = noise(key_list[5], (TOKENS, D), 1.0, 6.0, ((0, 16), (1, 16)))
    w_gate = noise(key_list[6], (EXPERTS, D, FW), D ** -0.5, 0.078125, ((0, 8), (2, 32)))
    w_up = noise(key_list[7], (EXPERTS, D, FW), D ** -0.5, 0.078125, ((0, 8), (2, 32)))
    w_down = noise(key_list[8], (EXPERTS, FW, D), FW ** -0.5, 0.0625, ((0, 8), (1, 32)))
    return {"hidden": hidden, "gain": gain, "expert_ids": expert_ids, "gate_weights": gate_weights, "segment_ids": segment_ids, "upstream": upstream, "w_gate": w_gate, "w_up": w_up, "w_down": w_down}


def expert_pass(operands):
    rows_in, cot_in, gate_mat, up_mat, down_mat = operands
    gate_pre = jnp.dot(rows_in, gate_mat, preferred_element_type=jnp.float32)
    up_proj = jnp.dot(rows_in, up_mat, preferred_element_type=jnp.float32)
    sigmoid_gate = jax.nn.sigmoid(gate_pre)
    activated = gate_pre * sigmoid_gate
    hidden_act = (activated * up_proj).astype(jnp.bfloat16)
    block_width = FW // (N_TP * N_GRP)

    def add_block(total, index):
        start = (index * block_width).astype(jnp.int32)
        act_block = lax.dynamic_slice_in_dim(hidden_act, start, block_width, 1)
        down_block = lax.dynamic_slice_in_dim(down_mat, start, block_width, 0)
        part = jnp.dot(act_block, down_block, preferred_element_type=jnp.float32).astype(jnp.bfloat16)
        return (total + part.astype(jnp.float32), None)
    start_total = jnp.zeros((rows_in.shape[0], down_mat.shape[1]), jnp.float32)
    out_total, unused = lax.scan(add_block, start_total, jnp.arange(N_TP * N_GRP, dtype=jnp.int32))
    expert_out = out_total.astype(jnp.bfloat16)
    grad_act = lax.dot_general(cot_in, down_mat, (((1,), (1,)), ((), ())), preferred_element_type=jnp.float32)
    grad_gate = (grad_act * up_proj * sigmoid_gate * (1.0 + gate_pre * (1.0 - sigmoid_gate))).astype(jnp.bfloat16)
    grad_up = (grad_act * activated).astype(jnp.bfloat16)
    grad_wgate = lax.dot_general(rows_in, grad_gate, (((0,), (0,)), ((), ())), preferred_element_type=jnp.float32)
    grad_wup = lax.dot_general(rows_in, grad_up, (((0,), (0,)), ((), ())), preferred_element_type=jnp.float32)
    grad_wdown = lax.dot_general(hidden_act, cot_in, (((0,), (0,)), ((), ())), preferred_element_type=jnp.float32)
    scores = lax.optimization_barrier(jnp.sum(jnp.abs(grad_wgate * gate_mat.astype(jnp.float32)), axis=0))
    scores = scores + lax.optimization_barrier(jnp.sum(jnp.abs(grad_wup * up_mat.astype(jnp.float32)), axis=0))
    scores = scores + lax.optimization_barrier(jnp.sum(jnp.abs(grad_wdown * down_mat.astype(jnp.float32)), axis=1))
    return (expert_out, scores)

def reference(hidden, gain, expert_ids, gate_weights, segment_ids, upstream, w_gate, w_up, w_down):
    wide_hidden = hidden.astype(jnp.float32)
    squares = lax.optimization_barrier(jnp.sum(wide_hidden * wide_hidden, axis=1, keepdims=True))
    normed = (wide_hidden * lax.rsqrt(squares / D + 1e-05) * gain.astype(jnp.float32)).astype(jnp.bfloat16)
    documents = jnp.arange(NDOCS, dtype=jnp.int32)
    doc_onehot = (segment_ids[:, None] == documents[None, :]).astype(jnp.float32)
    doc_len = lax.optimization_barrier(jnp.sum(doc_onehot, axis=0))
    tok_len = lax.optimization_barrier(jnp.sum(doc_onehot * doc_len[None, :], axis=1))
    tok_weight = RTOK / tok_len
    scaled = gate_weights * tok_weight[:, None]
    cot_rows = (scaled[:, :, None] * upstream.astype(jnp.float32)[:, None, :]).astype(jnp.bfloat16)
    shard_ids = expert_ids.reshape(TOKENS // RTOK, RTOK * TOP)
    onehot = (shard_ids[:, :, None] == jnp.arange(EXPERTS, dtype=jnp.int32)[None, None, :]).astype(jnp.int32)
    before = jnp.cumsum(onehot, axis=1).astype(jnp.int32) - onehot
    slot_ids = lax.optimization_barrier(jnp.sum(before * onehot, axis=2)).astype(jnp.int32).reshape(TOKENS, TOP)
    shard_index = (jnp.arange(TOKENS, dtype=jnp.int32) // RTOK).astype(jnp.int32)
    source_tok = shard_index // N_GRP
    source_grp = shard_index % N_GRP
    row_ids = (source_grp * (N_TOK * CAP) + source_tok * CAP)[:, None] + slot_ids
    row_ids = row_ids.astype(jnp.int32)
    rows_in = jnp.zeros((EXPERTS, ROWS, D), jnp.bfloat16)
    rows_in = rows_in.at[expert_ids, row_ids].set(jnp.broadcast_to(normed[:, None, :], (TOKENS, TOP, D)))
    cot_in = jnp.zeros((EXPERTS, ROWS, D), jnp.bfloat16)
    cot_in = cot_in.at[expert_ids, row_ids].set(cot_rows)
    expert_out, scores = lax.map(expert_pass, (rows_in, cot_in, w_gate, w_up, w_down))
    picked = expert_out[expert_ids, row_ids].astype(jnp.float32)
    mixed = (wide_hidden + lax.optimization_barrier(jnp.sum(gate_weights[:, :, None] * picked, axis=1))).astype(jnp.bfloat16)
    importance = scores / TOKENS
    return (mixed, importance)
```

```python
import functools
import math

import jax
import jax.numpy as jnp
from jax import lax
from jax.experimental import pallas as pl
from jax.experimental.pallas import tpu as pltpu
from jax.sharding import PartitionSpec as P

GAIN_ROWS = 16


def plane_shift(value, stage, step):
    side = math.isqrt(lax.axis_size("tp"))
    groups = lax.axis_size("grp")
    pairs = []
    for row in range(side):
        for col in range(side):
            for core in range(groups):
                if (core + stage) % 2 == 0:
                    target = row * side + (col + step) % side
                else:
                    target = ((row + step) % side) * side + col
                pairs.append(((row * side + col) * groups + core, target * groups + core))
    return lax.ppermute(value, ("tp", "grp"), pairs)


def swap_cores(value):
    return lax.ppermute(value, "grp", [(0, 1), (1, 0)])


def plane_gather(own):
    ahead = plane_shift(own, 0, -1)
    behind = plane_shift(own, 0, 1)
    across = plane_shift(own, 0, 2)
    low = jnp.stack([own, ahead])
    high = jnp.stack([across, behind])
    low_behind = plane_shift(low, 1, 1)
    low_ahead = plane_shift(low, 1, -1)
    high_ahead = plane_shift(high, 1, -1)
    high_behind = plane_shift(high, 1, 1)
    low_across = plane_shift(low_behind, 1, 1)
    high_across = plane_shift(high_ahead, 1, -1)
    pieces = [low, high, low_ahead, high_ahead, low_across, high_across, low_behind, high_behind]
    return jnp.concatenate(pieces, axis=0).reshape(4, 4, *own.shape)


def add_wide(*values):
    total = values[0].astype(jnp.float32)
    for value in values[1:]:
        total = total + value.astype(jnp.float32)
    return total.astype(jnp.bfloat16)


def plane_scatter(own, other):
    def piece(at, part):
        span = slice(2 * part, 2 * part + 2)
        return own[at, span], other[at, span]

    low_across = plane_shift(add_wide(*piece(2, 0)), 1, 1)
    high_across = plane_shift(add_wide(*piece(2, 1)), 1, -1)
    high_behind = plane_shift(add_wide(*piece(1, 1)), 1, 1)
    low_ahead = plane_shift(add_wide(*piece(3, 0)), 1, -1)
    low_behind = plane_shift(add_wide(*piece(1, 0), low_across), 1, 1)
    high_ahead = plane_shift(add_wide(*piece(3, 1), high_across), 1, -1)
    low = (low_behind, low_ahead)
    high = (high_behind, high_ahead)

    def column(at):
        received = low if at < 2 else high
        return add_wide(own[0, at], other[0, at], received[0][at % 2], received[1][at % 2])

    return add_wide(
        column(0),
        plane_shift(column(1), 0, 1),
        plane_shift(column(2), 0, 2),
        plane_shift(column(3), 0, -1),
    )


def document_lengths(counts):
    counts = counts + swap_cores(counts)
    size = lax.axis_size("tok")
    step = size // 2
    while step:
        pairs = [(i, (i + step) % size) for i in range(size)]
        counts = counts + lax.ppermute(counts, "tok", pairs)
        step //= 2
    return counts


def columns(x):
    return x[:, :128] + x[:, 128:256] + x[:, 256:384]


def forward_body(swapped, rows, width, table, x_ref, *refs):
    gate_refs, up_refs, down_refs = refs[0:4], refs[4:8], refs[8:12]
    act_ref, slope_ref, lin_ref, part_ref, gate_acc, up_acc, square_acc = refs[12:]
    step = pl.program_id(0)

    def block(ref, j):
        return ref.at[j, 0] if swapped else ref.at[0, j]

    @pl.when(step == 0)
    def _():
        gate_acc[...] = jnp.zeros_like(gate_acc)
        up_acc[...] = jnp.zeros_like(up_acc)
        square_acc[...] = jnp.zeros_like(square_acc)

    @pl.when(step < 4)
    def _():
        scaled, squares = [], square_acc[...]
        for j in range(4):
            wide = block(x_ref, j)[:rows, :].astype(jnp.float32)
            gain = block(x_ref, j)[rows:, :].astype(jnp.float32)[:1, :]
            squares = squares + columns(wide * wide)
            scaled.append((wide * gain).astype(jnp.bfloat16))
        square_acc[...] = squares
        left = jnp.concatenate(scaled, axis=1)
        gate = jnp.concatenate([r[...] for r in gate_refs], axis=0)
        up = jnp.concatenate([r[...] for r in up_refs], axis=0)
        gate_acc[...] += jnp.dot(left, gate, preferred_element_type=jnp.float32)
        up_acc[...] += jnp.dot(left, up, preferred_element_type=jnp.float32)

    @pl.when(step == 3)
    def _():
        total = jnp.sum(square_acc[...], axis=1, keepdims=True)
        scaling = lax.rsqrt(total / width + 1e-05)
        gate_pre = gate_acc[...] * scaling
        up_proj = up_acc[...] * scaling
        sigmoid_gate = jax.nn.sigmoid(gate_pre)
        activated = gate_pre * sigmoid_gate
        act_ref[...] = (activated * up_proj).astype(jnp.bfloat16)
        slope = up_proj * sigmoid_gate * (1.0 + gate_pre * (1.0 - sigmoid_gate))
        slope_ref[...] = slope * scaling
        lin_ref[...] = activated * scaling

    @pl.when(step >= 4)
    def _():
        for j in range(4):
            part = jnp.dot(act_ref[...], down_refs[j][...], preferred_element_type=jnp.float32)
            block(part_ref, j)[...] = part.astype(jnp.bfloat16)


def forward(gathered, swapped, table, gate_mat, up_mat, down_mat):
    padded, slice_width = gathered.shape[2:]
    rows = padded - GAIN_ROWS
    width, units = gate_mat.shape

    def first(s):
        return jnp.minimum(s, 3)

    def second(s):
        return jnp.maximum(s - 4, 0)

    def plane(at, count):
        if swapped:
            return pl.BlockSpec((4, 1, count, slice_width), lambda s, t: (0, at(s), 0, 0))
        return pl.BlockSpec((1, 4, count, slice_width), lambda s, t: (at(s), 0, 0, 0))

    row_specs = [
        pl.BlockSpec((slice_width, units), lambda s, t, j=j: (t[first(s) * 4 + j], 0)) for j in range(4)
    ]
    col_specs = [
        pl.BlockSpec((units, slice_width), lambda s, t, j=j: (0, t[second(s) * 4 + j])) for j in range(4)
    ]
    whole = pl.BlockSpec((rows, units), lambda s, t: (0, 0))
    wide = jax.ShapeDtypeStruct((rows, units), jnp.float32)
    return pl.pallas_call(
        functools.partial(forward_body, swapped, rows, width),
        out_shape=(
            jax.ShapeDtypeStruct((rows, units), jnp.bfloat16),
            wide,
            wide,
            jax.ShapeDtypeStruct((4, 4, rows, slice_width), jnp.bfloat16),
        ),
        grid_spec=pltpu.PrefetchScalarGridSpec(
            num_scalar_prefetch=1,
            grid=(8,),
            in_specs=[plane(first, padded)] + row_specs + row_specs + col_specs,
            out_specs=[whole, whole, whole, plane(second, rows)],
            scratch_shapes=[
                pltpu.VMEM((rows, units), jnp.float32),
                pltpu.VMEM((rows, units), jnp.float32),
                pltpu.VMEM((rows, 128), jnp.float32),
            ],
        ),
        compiler_params=pltpu.CompilerParams(vmem_limit_bytes=48 << 20),
        cost_estimate=pl.CostEstimate(
            flops=6 * rows * width * units, transcendentals=rows * units, bytes_accessed=18 << 20
        ),
        name="forward",
    )(table, gathered, *([gate_mat] * 4), *([up_mat] * 4), *([down_mat] * 4))


def backward_body(rows, table, xo_ref, xp_ref, co_ref, cp_ref, *refs):
    down_refs, gate_refs, up_refs = refs[0:4], refs[4:8], refs[8:12]
    act_o, act_p, slope_o, slope_p, lin_o, lin_p = refs[12:18]
    out_ref, grad_acc, left_acc, act_acc = refs[18:]
    step = pl.program_id(0)

    @pl.when(step == 0)
    def _():
        grad_acc[...] = jnp.zeros_like(grad_acc)
        out_ref[...] = jnp.zeros_like(out_ref)

    @pl.when(step < 4)
    def _():
        own = jnp.concatenate([co_ref[0, j] for j in range(4)], axis=1)
        other = jnp.concatenate([cp_ref[j, 0] for j in range(4)], axis=1)
        down = jnp.concatenate([r[...] for r in down_refs], axis=1)
        dims = (((1,), (1,)), ((), ()))
        grad_acc[:rows, :] += lax.dot_general(own, down, dims, preferred_element_type=jnp.float32)
        grad_acc[rows:, :] += lax.dot_general(other, down, dims, preferred_element_type=jnp.float32)

    @pl.when(step == 3)
    def _():
        units = grad_acc.shape[1]
        grad = grad_acc[...]
        slope = jnp.concatenate([slope_o[...], slope_p[...]], axis=0)
        lin = jnp.concatenate([lin_o[...], lin_p[...]], axis=0)
        left_acc[:units, :] = (grad * slope).T.astype(jnp.bfloat16)
        left_acc[units:, :] = (grad * lin).T.astype(jnp.bfloat16)
        act = jnp.concatenate([act_o[...], act_p[...]], axis=0).astype(jnp.float32)
        act_acc[...] = act.T.astype(jnp.bfloat16)

    @pl.when(step >= 4)
    def _():
        units = grad_acc.shape[1]
        total = out_ref[...]
        for j in range(4):
            gain = xo_ref[0, j, rows:, :].astype(jnp.float32)[:1, :]
            right = jnp.concatenate([xo_ref[0, j, :rows, :], xp_ref[j, 0, :rows, :]], axis=0)
            grads = jnp.dot(left_acc[...], right, preferred_element_type=jnp.float32)
            gate = jnp.abs(grads[:units, :] * gate_refs[j][...].astype(jnp.float32))
            up = jnp.abs(grads[units:, :] * up_refs[j][...].astype(jnp.float32))
            total = total + columns((gate + up) * jnp.abs(gain))
            right = jnp.concatenate([co_ref[0, j], cp_ref[j, 0]], axis=0)
            grads = jnp.dot(act_acc[...], right, preferred_element_type=jnp.float32)
            total = total + columns(jnp.abs(grads * down_refs[j][...].astype(jnp.float32)))
        out_ref[...] = total


def backward(table, rows_own, rows_other, cot_own, cot_other, down_mat, gate_cols, up_cols, saved):
    padded, slice_width = rows_own.shape[2:]
    rows = padded - GAIN_ROWS
    units, width = down_mat.shape

    def late(s):
        return jnp.maximum(s - 4, 0)

    def both(s):
        return lax.rem(s, 4)

    def plane(at, count, swapped):
        if swapped:
            return pl.BlockSpec((4, 1, count, slice_width), lambda s, t: (0, at(s), 0, 0))
        return pl.BlockSpec((1, 4, count, slice_width), lambda s, t: (at(s), 0, 0, 0))

    def col_specs(at):
        return [
            pl.BlockSpec((units, slice_width), lambda s, t, j=j: (0, t[at(s) * 4 + j])) for j in range(4)
        ]

    whole = pl.BlockSpec((rows, units), lambda s, t: (0, 0))
    return pl.pallas_call(
        functools.partial(backward_body, rows),
        out_shape=jax.ShapeDtypeStruct((units, 128), jnp.float32),
        grid_spec=pltpu.PrefetchScalarGridSpec(
            num_scalar_prefetch=1,
            grid=(8,),
            in_specs=[
                plane(late, padded, False),
                plane(late, padded, True),
                plane(both, rows, False),
                plane(both, rows, True),
            ]
            + col_specs(both)
            + col_specs(late)
            + col_specs(late)
            + [whole] * 6,
            out_specs=pl.BlockSpec((units, 128), lambda s, t: (0, 0)),
            scratch_shapes=[
                pltpu.VMEM((2 * rows, units), jnp.float32),
                pltpu.VMEM((2 * units, 2 * rows), jnp.bfloat16),
                pltpu.VMEM((units, 2 * rows), jnp.bfloat16),
            ],
        ),
        compiler_params=pltpu.CompilerParams(vmem_limit_bytes=56 << 20),
        cost_estimate=pl.CostEstimate(
            flops=16 * rows * width * units, transcendentals=0, bytes_accessed=36 << 20
        ),
        name="backward",
    )(
        table,
        rows_own,
        rows_other,
        cot_own,
        cot_other,
        *([down_mat] * 4),
        *([gate_cols] * 4),
        *([up_cols] * 4),
        *saved,
    )


def on_device(hidden, gain, expert_ids, gate_weights, segment_ids, upstream, w_gate, w_up, w_down):
    rows_here, slice_width = hidden.shape
    top_count = expert_ids.shape[1]
    experts = lax.axis_size("tok")
    groups = lax.axis_size("grp")
    capacity = 5 * rows_here // (2 * experts)
    side = math.isqrt(lax.axis_size("tp"))
    place = lax.axis_index("tp")
    row_at, col_at = place // side, place % side
    outer = jnp.arange(side * side, dtype=jnp.int32) // side
    inner = jnp.arange(side * side, dtype=jnp.int32) % side
    first_core = lax.axis_index("grp") == 0
    row_step = jnp.where(first_core, outer, inner)
    col_step = jnp.where(first_core, inner, outer)
    table = (row_at + row_step) % side * side + (col_at + col_step) % side

    onehot = (
        expert_ids.reshape(-1)[:, None] == jnp.arange(experts, dtype=jnp.int32)[None, :]
    ).astype(jnp.int32)
    before = jnp.cumsum(onehot, axis=0) - onehot
    slot_ids = jnp.sum(before * onehot, axis=1).reshape(rows_here, top_count)
    targets = expert_ids * capacity + slot_ids
    all_slots = jnp.arange(experts * capacity, dtype=jnp.int32)
    matches = all_slots[:, None, None] == targets[None, :, :]
    placing = jnp.any(matches, axis=2).astype(jnp.bfloat16)

    def to_experts(block):
        block = block.reshape(experts, capacity, slice_width)
        came = lax.all_to_all(block, "tok", split_axis=0, concat_axis=0, tiled=True)
        return came.reshape(experts * capacity, slice_width)

    block_rows = jnp.dot(placing, hidden, preferred_element_type=jnp.float32).astype(jnp.bfloat16)
    gain_rows = jnp.broadcast_to(gain[None, :], (GAIN_ROWS, slice_width))
    rows_own = plane_gather(jnp.concatenate([to_experts(block_rows), gain_rows], axis=0))
    rows_other = swap_cores(rows_own)

    documents = jnp.arange(experts * groups, dtype=jnp.int32)
    doc_onehot = (segment_ids[:, None] == documents[None, :]).astype(jnp.float32)
    doc_len = document_lengths(jnp.sum(doc_onehot, axis=0))
    tok_len = jnp.sum(doc_onehot * doc_len[None, :], axis=1)
    tok_weight = rows_here / tok_len
    scaled = gate_weights * tok_weight[:, None]
    slot_scale = jnp.sum(jnp.where(matches, scaled[None, :, :], 0.0), axis=(1, 2))
    combining = jnp.sum(jnp.where(matches, gate_weights[None, :, :], 0.0), axis=2)
    block_cot = jnp.dot(placing, upstream, preferred_element_type=jnp.float32) * slot_scale[:, None]
    cot_own = plane_gather(to_experts(block_cot.astype(jnp.bfloat16)))
    cot_other = swap_cores(cot_own)

    gate_mat, up_mat, down_mat = w_gate[0], w_up[0], w_down[0]
    act_own, slope_own, lin_own, part_own = forward(
        rows_own, False, table, gate_mat, up_mat, down_mat
    )
    act_other, slope_other, lin_other, part_other = forward(
        rows_other, True, table, gate_mat, up_mat, down_mat
    )
    outgoing = plane_scatter(part_own, swap_cores(part_other))

    saved = (act_own, act_other, slope_own, slope_other, lin_own, lin_other)
    scores = backward(
        table, rows_own, rows_other, cot_own, cot_other, down_mat, gate_mat.T, up_mat.T, saved
    )
    importance = jnp.sum(scores, axis=1) / (rows_here * experts * groups)

    returned = to_experts(outgoing).astype(jnp.float32)
    combined = jnp.dot(
        combining.T, returned, precision=lax.Precision.HIGHEST, preferred_element_type=jnp.float32
    )
    mixed = (hidden.astype(jnp.float32) + combined).astype(jnp.bfloat16)
    return (mixed, importance[None, :])


def solution(mesh):
    placed = (
        P(("tok", "grp"), "tp"),
        P("tp"),
        P(("tok", "grp"), None),
        P(("tok", "grp"), None),
        P(("tok", "grp")),
        P(("tok", "grp"), "tp"),
        P("tok", None, ("tp", "grp")),
        P("tok", None, ("tp", "grp")),
        P("tok", ("tp", "grp"), None),
    )
    return jax.shard_map(
        on_device,
        mesh=mesh,
        in_specs=placed,
        out_specs=(P(("tok", "grp"), "tp"), P("tok", ("tp", "grp"))),
        check_vma=False,
    )
```

```python
import functools
import math

import jax
import jax.numpy as jnp
from jax import lax
from jax.experimental import pallas as pl
from jax.experimental.pallas import tpu as pltpu
from jax.sharding import PartitionSpec as P


GAIN_ROWS = 16
VMEM_LIMIT = 16 << 20
SCORE_STEPS = ((0, 3), (3, 3), (6, 2))


def plane_shift(value, stage, step):
    side = math.isqrt(lax.axis_size("tp"))
    groups = lax.axis_size("grp")
    pairs = []
    for row in range(side):
        for col in range(side):
            for core in range(groups):
                if (core + stage) % 2 == 0:
                    target = row * side + (col + step) % side
                else:
                    target = ((row + step) % side) * side + col
                pairs.append(((row * side + col) * groups + core, target * groups + core))
    return lax.ppermute(value, ("tp", "grp"), pairs)


def swap_cores(value):
    return lax.ppermute(value, "grp", [(0, 1), (1, 0)])


def plane_gather(own):
    ahead = plane_shift(own, 0, -1)
    behind = plane_shift(own, 0, 1)
    across = plane_shift(own, 0, 2)
    low = jnp.stack([own, ahead])
    high = jnp.stack([across, behind])
    low_behind = plane_shift(low, 1, 1)
    low_ahead = plane_shift(low, 1, -1)
    high_ahead = plane_shift(high, 1, -1)
    high_behind = plane_shift(high, 1, 1)
    low_across = plane_shift(low_behind, 1, 1)
    high_across = plane_shift(high_ahead, 1, -1)
    return [low, high, low_ahead, high_ahead, low_across, high_across, low_behind, high_behind]


def add_wide(*values):
    total = values[0].astype(jnp.float32)
    for value in values[1:]:
        total = total + value.astype(jnp.float32)
    return total.astype(jnp.bfloat16)


def plane_scatter(own, other):
    def piece(at, part):
        span = slice(2 * part, 2 * part + 2)
        return own[at, span], other[at][span]

    low_across = plane_shift(add_wide(*piece(2, 0)), 1, 1)
    high_across = plane_shift(add_wide(*piece(2, 1)), 1, -1)
    to_behind, to_ahead = add_wide(*piece(1, 1)), add_wide(*piece(3, 0))
    high_behind = plane_shift(to_behind, 1, 1)
    low_ahead = plane_shift(to_ahead, 1, -1)
    low_across, _ = lax.optimization_barrier((low_across, to_behind))
    high_across, _ = lax.optimization_barrier((high_across, to_ahead))
    low_behind = plane_shift(add_wide(*piece(1, 0), low_across), 1, 1)
    high_ahead = plane_shift(add_wide(*piece(3, 1), high_across), 1, -1)
    low = (low_behind, low_ahead)
    high = (high_behind, high_ahead)

    def column(at):
        received = low if at < 2 else high
        return add_wide(own[0, at], other[0][at], received[0][at % 2], received[1][at % 2])

    return add_wide(
        column(0),
        plane_shift(column(1), 0, 1),
        plane_shift(column(2), 0, 2),
        plane_shift(column(3), 0, -1),
    )


def columns(x):
    return x[:, :128] + x[:, 128:256] + x[:, 256:384]


def column_specs(units, slice_width, at, which=0):
    return [
        pl.BlockSpec((units, slice_width), lambda s, *t, j=j: (0, t[which][at(s) * 2 + j]))
        for j in range(2)
    ]


def forward_body(rows, width, table, *refs):
    pieces, gate_refs, up_refs, scale_ref = refs[0:8], refs[8:10], refs[10:12], refs[12]
    act_ref, left_ref, slope_ref, lin_ref = refs[13:17]
    gate_acc, up_acc, square_acc, held, sems = refs[17:]
    step = pl.program_id(0)

    def copy(piece, at):
        span = piece.at[:, pl.ds(0, rows + GAIN_ROWS), :]
        return pltpu.make_async_copy(span, held.at[at], sems.at[at])

    @pl.when(step == 0)
    def _():
        for at, piece in enumerate(pieces):
            copy(piece, at).start()
        gate_acc[...] = jnp.zeros_like(gate_acc)
        up_acc[...] = jnp.zeros_like(up_acc)
        square_acc[...] = jnp.zeros_like(square_acc)

    copy(pieces[0], step).wait()
    scaled, squares = [], square_acc[...]
    for j in range(2):
        wide = held[step, j, :rows, :].astype(jnp.float32)
        gain = held[step, j, rows:, :].astype(jnp.float32)[:1, :]
        squares = squares + columns(wide * wide)
        scaled.append((wide * gain).astype(jnp.bfloat16))
    square_acc[...] = squares
    left = jnp.concatenate(scaled, axis=1)
    gate = jnp.concatenate([r[...] for r in gate_refs], axis=0)
    up = jnp.concatenate([r[...] for r in up_refs], axis=0)
    gate_acc[...] += jnp.dot(left, gate, preferred_element_type=jnp.float32)
    up_acc[...] += jnp.dot(left, up, preferred_element_type=jnp.float32)

    @pl.when(step == 7)
    def _():
        total = jnp.sum(square_acc[...], axis=1, keepdims=True)
        scaling = lax.rsqrt(total / width + 1e-05)
        gate_pre = gate_acc[...] * scaling
        up_proj = up_acc[...] * scaling
        sigmoid_gate = jax.nn.sigmoid(gate_pre)
        activated = gate_pre * sigmoid_gate
        act = (activated * up_proj).astype(jnp.bfloat16)
        act_ref[...] = act
        left_ref[...] = (act.astype(jnp.float32) * scale_ref[...]).astype(jnp.bfloat16)
        slope = up_proj * sigmoid_gate * (1.0 + gate_pre * (1.0 - sigmoid_gate))
        scaling = scaling * scale_ref[...]
        slope_ref[...] = slope * scaling
        lin_ref[...] = activated * scaling


def forward(pieces, table, gate_mat, up_mat, row_scale):
    slice_width = pieces[0].shape[2]
    rows = row_scale.shape[0]
    width, units = gate_mat.shape
    row_specs = [
        pl.BlockSpec((slice_width, units), lambda s, t, j=j: (t[s * 2 + j], 0)) for j in range(2)
    ]
    whole = pl.BlockSpec((rows, units), lambda s, t: (0, 0))
    wide = jax.ShapeDtypeStruct((rows, units), jnp.float32)
    narrow = jax.ShapeDtypeStruct((rows, units), jnp.bfloat16)
    return pl.pallas_call(
        functools.partial(forward_body, rows, width),
        out_shape=(narrow, narrow, wide, wide),
        grid_spec=pltpu.PrefetchScalarGridSpec(
            num_scalar_prefetch=1,
            grid=(8,),
            in_specs=[pl.BlockSpec(memory_space=pl.ANY)] * 8
            + row_specs
            + row_specs
            + [pl.BlockSpec((rows, 1), lambda s, t: (0, 0))],
            out_specs=[whole, whole, whole, whole],
            scratch_shapes=[
                pltpu.VMEM((rows, units), jnp.float32),
                pltpu.VMEM((rows, units), jnp.float32),
                pltpu.VMEM((rows, 128), jnp.float32),
                pltpu.VMEM((8, 2, rows + GAIN_ROWS, slice_width), jnp.bfloat16),
                pltpu.SemaphoreType.DMA((8,)),
            ],
        ),
        compiler_params=pltpu.CompilerParams(vmem_limit_bytes=VMEM_LIMIT),
        cost_estimate=pl.CostEstimate(
            flops=4 * rows * width * units, transcendentals=rows * units, bytes_accessed=11 << 20
        ),
        name="forward",
    )(table, *pieces, *([gate_mat] * 2), *([up_mat] * 2), row_scale)


def down_body(table, act_ref, low_ref, high_ref, part_ref):
    for j, ref in enumerate((low_ref, high_ref)):
        part = jnp.dot(act_ref[...], ref[...], preferred_element_type=jnp.float32)
        part_ref[0, j] = part.astype(jnp.bfloat16)


def down(act, table, first, count, down_mat):
    rows, units = act.shape
    slice_width = down_mat.shape[1] // 16

    def at(s):
        return s + 2 * first

    return pl.pallas_call(
        down_body,
        out_shape=jax.ShapeDtypeStruct((count, 4, rows, slice_width), jnp.bfloat16),
        grid_spec=pltpu.PrefetchScalarGridSpec(
            num_scalar_prefetch=1,
            grid=(2 * count,),
            in_specs=[pl.BlockSpec((rows, units), lambda s, t: (0, 0))]
            + column_specs(units, slice_width, at),
            out_specs=pl.BlockSpec((1, 2, rows, slice_width), lambda s, t: (s // 2, s % 2, 0, 0)),
        ),
        compiler_params=pltpu.CompilerParams(vmem_limit_bytes=VMEM_LIMIT),
        cost_estimate=pl.CostEstimate(
            flops=8 * count * rows * units * slice_width,
            transcendentals=0,
            bytes_accessed=count * (2 << 20),
        ),
        name="down",
    )(table, act, down_mat, down_mat)


def grads_body(rows, table, other_table, *refs):
    pieces, own_refs, other_refs = refs[0:16], refs[16:18], refs[18:20]
    act_o, act_p, slope_o, slope_p, lin_o, lin_p = refs[20:26]
    left_ref, acts_ref, grad_acc, held, sems = refs[26:]
    step = pl.program_id(0)

    def copy(piece, at):
        span = piece.at[:, pl.ds(rows + GAIN_ROWS, rows), :]
        return pltpu.make_async_copy(span, held.at[at], sems.at[at])

    @pl.when(step == 0)
    def _():
        for at in range(8):
            copy(pieces[at], at).start()
            copy(pieces[at + 8], at + 8).start()
        grad_acc[...] = jnp.zeros_like(grad_acc)

    dims = (((1,), (1,)), ((), ()))
    copy(pieces[0], step).wait()
    cot = jnp.concatenate([held[step, j] for j in range(2)], axis=1)
    mat = jnp.concatenate([r[...] for r in own_refs], axis=1)
    grad_acc[:rows, :] += lax.dot_general(cot, mat, dims, preferred_element_type=jnp.float32)
    copy(pieces[0], step + 8).wait()
    cot = jnp.concatenate([held[step + 8, j] for j in range(2)], axis=1)
    mat = jnp.concatenate([r[...] for r in other_refs], axis=1)
    grad_acc[rows:, :] += lax.dot_general(cot, mat, dims, preferred_element_type=jnp.float32)

    @pl.when(step == 7)
    def _():
        units = grad_acc.shape[1]
        grad = grad_acc[...]
        slope = jnp.concatenate([slope_o[...], slope_p[...]], axis=0)
        lin = jnp.concatenate([lin_o[...], lin_p[...]], axis=0)
        left_ref[:units, :] = (grad * slope).T.astype(jnp.bfloat16)
        left_ref[units:, :] = (grad * lin).T.astype(jnp.bfloat16)
        act = jnp.concatenate([act_o[...], act_p[...]], axis=0).astype(jnp.float32)
        acts_ref[...] = act.T.astype(jnp.bfloat16)


def activation_grads(tables, pieces, down_mat, saved):
    rows = saved[0].shape[0]
    slice_width = pieces[0].shape[2]
    units, width = down_mat.shape
    whole = pl.BlockSpec((rows, units), lambda s, *t: (0, 0))

    def at(s):
        return s

    return pl.pallas_call(
        functools.partial(grads_body, rows),
        out_shape=(
            jax.ShapeDtypeStruct((2 * units, 2 * rows), jnp.bfloat16),
            jax.ShapeDtypeStruct((units, 2 * rows), jnp.bfloat16),
        ),
        grid_spec=pltpu.PrefetchScalarGridSpec(
            num_scalar_prefetch=2,
            grid=(8,),
            in_specs=[pl.BlockSpec(memory_space=pl.ANY)] * 16
            + column_specs(units, slice_width, at, 0)
            + column_specs(units, slice_width, at, 1)
            + [whole] * 6,
            out_specs=[
                pl.BlockSpec((2 * units, 2 * rows), lambda s, *t: (0, 0)),
                pl.BlockSpec((units, 2 * rows), lambda s, *t: (0, 0)),
            ],
            scratch_shapes=[
                pltpu.VMEM((2 * rows, units), jnp.float32),
                pltpu.VMEM((16, 2, rows, slice_width), jnp.bfloat16),
                pltpu.SemaphoreType.DMA((16,)),
            ],
        ),
        compiler_params=pltpu.CompilerParams(vmem_limit_bytes=VMEM_LIMIT + (4 << 20)),
        cost_estimate=pl.CostEstimate(
            flops=4 * rows * width * units, transcendentals=0, bytes_accessed=14 << 20
        ),
        name="grads",
    )(*tables, *pieces, *([down_mat] * 4), *saved)


def score_body(rows, start, steps, table, left_ref, acts_ref, *refs):
    places = score_pieces(start, steps)
    pieces = dict(zip(places, refs[: len(places)], strict=True))
    refs = refs[len(places) :]
    down_refs, gate_refs, up_refs, out_ref = refs[0:2], refs[2:4], refs[4:6], refs[6]
    own_held, other_held, own_sems, other_sems = refs[7:]
    here = pl.program_id(0)

    @pl.when(here == 0)
    def _():
        for at in range(steps):
            i, h = divmod(start + at, 2)
            pltpu.make_async_copy(
                pieces[0, start + at], own_held.at[at], own_sems.at[at]
            ).start()
            for j in range(2):
                source = pieces[1, 2 * (2 * h + j) + i // 2].at[i % 2]
                pltpu.make_async_copy(source, other_held.at[at, j], other_sems.at[at, j]).start()
        out_ref[...] = jnp.zeros_like(out_ref)

    pltpu.make_async_copy(pieces[0, start], own_held.at[here], own_sems.at[here]).wait()
    units = acts_ref.shape[0]
    cots = rows + GAIN_ROWS
    total = out_ref[...]
    for j in range(2):
        source = pieces[0, start].at[j]
        pltpu.make_async_copy(source, other_held.at[here, j], other_sems.at[here, j]).wait()
        gain = own_held[here, j, rows:cots, :].astype(jnp.float32)[:1, :]
        right = jnp.concatenate([own_held[here, j, :rows, :], other_held[here, j, :rows, :]], axis=0)
        grads = jnp.dot(left_ref[...], right, preferred_element_type=jnp.float32)
        gate = jnp.abs(grads[:units, :] * gate_refs[j][...].astype(jnp.float32))
        up = jnp.abs(grads[units:, :] * up_refs[j][...].astype(jnp.float32))
        total = total + columns((gate + up) * jnp.abs(gain))
        right = jnp.concatenate([own_held[here, j, cots:, :], other_held[here, j, cots:, :]], axis=0)
        grads = jnp.dot(acts_ref[...], right, preferred_element_type=jnp.float32)
        total = total + columns(jnp.abs(grads * down_refs[j][...].astype(jnp.float32)))
    out_ref[...] = total


def score_pieces(start, steps):
    places = [(0, start + at) for at in range(steps)]
    for at in range(steps):
        i, h = divmod(start + at, 2)
        for j in range(2):
            place = (1, 2 * (2 * h + j) + i // 2)
            if place not in places:
                places.append(place)
    return places


def score(start, steps, table, lefts, pieces, mats):
    total_rows, slice_width = pieces[0].shape[1:]
    rows = (total_rows - GAIN_ROWS) // 2
    units = lefts[1].shape[0]
    used = [pieces[8 * side + number] for side, number in score_pieces(start, steps)]

    def at(s):
        return s + start

    down_mat, gate_cols, up_cols = mats
    columns_of = column_specs(units, slice_width, at)
    return pl.pallas_call(
        functools.partial(score_body, rows, start, steps),
        out_shape=jax.ShapeDtypeStruct((units, 128), jnp.float32),
        grid_spec=pltpu.PrefetchScalarGridSpec(
            num_scalar_prefetch=1,
            grid=(steps,),
            in_specs=[
                pl.BlockSpec((2 * units, 2 * rows), lambda s, t: (0, 0)),
                pl.BlockSpec((units, 2 * rows), lambda s, t: (0, 0)),
            ]
            + [pl.BlockSpec(memory_space=pl.ANY)] * len(used)
            + columns_of
            + columns_of
            + columns_of,
            out_specs=pl.BlockSpec((units, 128), lambda s, t: (0, 0)),
            scratch_shapes=[
                pltpu.VMEM((steps, 2, total_rows, slice_width), jnp.bfloat16),
                pltpu.VMEM((steps, 2, total_rows, slice_width), jnp.bfloat16),
                pltpu.SemaphoreType.DMA((steps,)),
                pltpu.SemaphoreType.DMA((steps, 2)),
            ],
        ),
        compiler_params=pltpu.CompilerParams(vmem_limit_bytes=VMEM_LIMIT),
        cost_estimate=pl.CostEstimate(
            flops=12 * rows * units * slice_width * 2 * steps,
            transcendentals=0,
            bytes_accessed=steps * (5 << 19),
        ),
        name="score",
    )(
        table,
        *lefts,
        *used,
        *([down_mat] * 2),
        *([gate_cols] * 2),
        *([up_cols] * 2),
    )


def turn_body(gate_ref, up_ref, gate_out, up_out):
    gate_out[...] = gate_ref[...].T
    up_out[...] = up_ref[...].T


def turned(gate_mat, up_mat):
    width, units = gate_mat.shape
    count = 8
    tall = pl.BlockSpec((width // count, units), lambda s: (s, 0))
    flat = pl.BlockSpec((units, width // count), lambda s: (0, s))
    shape = jax.ShapeDtypeStruct((units, width), gate_mat.dtype)
    return pl.pallas_call(
        turn_body,
        out_shape=(shape, shape),
        grid=(count,),
        in_specs=[tall, tall],
        out_specs=[flat, flat],
        compiler_params=pltpu.CompilerParams(vmem_limit_bytes=VMEM_LIMIT),
        cost_estimate=pl.CostEstimate(flops=0, transcendentals=0, bytes_accessed=12 << 20),
        name="turn",
    )(gate_mat, up_mat)


def on_device(hidden, gain, expert_ids, gate_weights, segment_ids, upstream, w_gate, w_up, w_down):
    rows_here, slice_width = hidden.shape
    top_count = expert_ids.shape[1]
    experts = lax.axis_size("tok")
    groups = lax.axis_size("grp")
    capacity = 5 * rows_here // (2 * experts)
    side = math.isqrt(lax.axis_size("tp"))
    place = lax.axis_index("tp")
    row_at, col_at = place // side, place % side
    outer = jnp.arange(side * side, dtype=jnp.int32) // side
    inner = jnp.arange(side * side, dtype=jnp.int32) % side
    first_core = lax.axis_index("grp") == 0
    row_step = jnp.where(first_core, outer, inner)
    col_step = jnp.where(first_core, inner, outer)
    table = (row_at + row_step) % side * side + (col_at + col_step) % side
    other_table = (row_at + col_step) % side * side + (col_at + row_step) % side

    documents = jnp.arange(experts * groups, dtype=jnp.int32)
    doc_onehot = (segment_ids[:, None] == documents[None, :]).astype(jnp.float32)
    counts = jnp.sum(doc_onehot, axis=0)

    onehot = (
        expert_ids.reshape(-1)[:, None] == jnp.arange(experts, dtype=jnp.int32)[None, :]
    ).astype(jnp.int32)
    before = jnp.cumsum(onehot, axis=0) - onehot
    slot_ids = jnp.sum(before * onehot, axis=1).reshape(rows_here, top_count)

    def matches_of(stride):
        targets = expert_ids * stride + slot_ids
        all_slots = jnp.arange(experts * stride, dtype=jnp.int32)
        return all_slots[:, None, None] == targets[None, :, :]

    def to_experts(block, stride):
        block = block.reshape(experts, stride, slice_width)
        return lax.all_to_all(block, "tok", split_axis=0, concat_axis=0, tiled=True)

    stride = 2 * capacity + 8
    at_slot = jnp.arange(experts * stride, dtype=jnp.int32)
    tokens = jnp.concatenate([hidden, upstream], axis=0)
    targets = expert_ids * stride + slot_ids
    targets = jnp.concatenate([targets, targets + capacity], axis=0)
    placing = jnp.any(at_slot[:, None, None] == targets[None, :, :], axis=2).astype(jnp.bfloat16)
    count_lanes = jnp.pad(counts, (0, slice_width - counts.shape[0]))
    count_rows = jnp.where(
        at_slot[:, None] % stride == 2 * capacity, count_lanes[None, :], 0.0
    )
    blocks = jnp.dot(placing, tokens, preferred_element_type=jnp.float32) + count_rows
    came = to_experts(blocks.astype(jnp.bfloat16), stride)
    came_rows = came[:, :capacity].reshape(experts * capacity, slice_width)
    came_cot = came[:, capacity : 2 * capacity].reshape(experts * capacity, slice_width)
    gain_rows = jnp.broadcast_to(gain[None, :], (GAIN_ROWS, slice_width))
    own_pieces = plane_gather(jnp.concatenate([came_rows, gain_rows, came_cot], axis=0))
    other_pieces = [swap_cores(piece) for piece in own_pieces]

    doc_half = jnp.sum(came[:, 2 * capacity, : counts.shape[0]].astype(jnp.float32), axis=0)
    doc_len = doc_half + swap_cores(doc_half)
    tok_len = jnp.sum(doc_onehot * doc_len[None, :], axis=1)
    tok_weight = rows_here / tok_len
    scaled = gate_weights * tok_weight[:, None]
    matches = matches_of(capacity)
    slot_scale = jnp.sum(jnp.where(matches, scaled[None, :, :], 0.0), axis=(1, 2))
    combining = jnp.sum(jnp.where(matches, gate_weights[None, :, :], 0.0), axis=2)
    scale_own = lax.all_to_all(
        slot_scale.reshape(experts, capacity), "tok", split_axis=0, concat_axis=0, tiled=True
    )
    scale_other = swap_cores(scale_own).reshape(-1, 1)
    scale_own = scale_own.reshape(-1, 1)

    gate_mat, up_mat, down_mat = w_gate[0], w_up[0], w_down[0]
    gate_cols, up_cols = turned(gate_mat, up_mat)
    act_own, left_own, slope_own, lin_own = forward(own_pieces, table, gate_mat, up_mat, scale_own)
    part_own = down(act_own, table, 0, 4, down_mat)
    act_other, left_other, slope_other, lin_other = forward(
        other_pieces, other_table, gate_mat, up_mat, scale_other
    )
    part_other = {}
    for at in (2, 1, 3, 0):
        part = down(act_other, other_table, at, 1, down_mat)
        part_other[at] = swap_cores(part[0])
    outgoing = plane_scatter(part_own, part_other)

    saved = (left_own, left_other, slope_own, slope_other, lin_own, lin_other)
    lefts = activation_grads(
        (table, other_table), own_pieces + other_pieces, down_mat, saved
    )
    scores = 0.0
    for start, steps in SCORE_STEPS:
        scores = scores + score(
            start,
            steps,
            table,
            lefts,
            own_pieces + other_pieces,
            (down_mat, gate_cols, up_cols),
        )
    importance = jnp.sum(scores, axis=1) / (rows_here * experts * groups)

    returned = to_experts(outgoing, capacity)
    returned = returned.reshape(experts * capacity, slice_width).astype(jnp.float32)
    combined = jnp.dot(
        combining.T, returned, precision=lax.Precision.HIGHEST, preferred_element_type=jnp.float32
    )
    mixed = (hidden.astype(jnp.float32) + combined).astype(jnp.bfloat16)
    return (mixed, importance[None, :])


def solution(mesh):
    placed = (
        P(("tok", "grp"), "tp"),
        P("tp"),
        P(("tok", "grp"), None),
        P(("tok", "grp"), None),
        P(("tok", "grp")),
        P(("tok", "grp"), "tp"),
        P("tok", None, ("tp", "grp")),
        P("tok", None, ("tp", "grp")),
        P("tok", ("tp", "grp"), None),
    )
    return jax.shard_map(
        on_device,
        mesh=mesh,
        in_specs=placed,
        out_specs=(P(("tok", "grp"), "tp"), P("tok", ("tp", "grp"))),
        check_vma=False,
    )
```

```python
import functools
import math

import jax
import jax.numpy as jnp
from jax import lax
from jax.experimental import pallas as pl
from jax.experimental.pallas import tpu as pltpu
from jax.sharding import PartitionSpec as P


GAIN_ROWS = 16
VMEM_LIMIT = 16 << 20
EARLY = (0, 1, 6, 3)
LATE = (2, 7, 4, 5)
SCORE_STEPS = ((0, 3), (3, 4), (7, 1))


def plane_shift(value, stage, step):
    side = math.isqrt(lax.axis_size("tp"))
    groups = lax.axis_size("grp")
    pairs = []
    for row in range(side):
        for col in range(side):
            for core in range(groups):
                if (core + stage) % 2 == 0:
                    target = row * side + (col + step) % side
                else:
                    target = ((row + step) % side) * side + col
                pairs.append(((row * side + col) * groups + core, target * groups + core))
    return lax.ppermute(value, ("tp", "grp"), pairs)


def swap_cores(value):
    return lax.ppermute(value, "grp", [(0, 1), (1, 0)])


def plane_gather(own):
    ahead = plane_shift(own, 0, -1)
    behind = plane_shift(own, 0, 1)
    across = plane_shift(own, 0, 2)
    low = jnp.stack([own, ahead])
    high = jnp.stack([across, behind])
    low_behind = plane_shift(low, 1, 1)
    low_ahead = plane_shift(low, 1, -1)
    high_ahead = plane_shift(high, 1, -1)
    high_behind = plane_shift(high, 1, 1)
    low_across = plane_shift(low_behind, 1, 1)
    high_across = plane_shift(high_ahead, 1, -1)
    return [low, high, low_ahead, high_ahead, low_across, high_across, low_behind, high_behind]


def add_wide(*values):
    total = values[0].astype(jnp.float32)
    for value in values[1:]:
        total = total + value.astype(jnp.float32)
    return total.astype(jnp.bfloat16)


def plane_scatter(own, other):
    def piece(at, part):
        span = slice(2 * part, 2 * part + 2)
        return own[at, span], other[at][span]

    low_across = plane_shift(add_wide(*piece(2, 0)), 1, 1)
    high_across = plane_shift(add_wide(*piece(2, 1)), 1, -1)
    to_behind, to_ahead = add_wide(*piece(1, 1)), add_wide(*piece(3, 0))
    high_behind = plane_shift(to_behind, 1, 1)
    low_ahead = plane_shift(to_ahead, 1, -1)
    low_across, _ = lax.optimization_barrier((low_across, to_behind))
    high_across, _ = lax.optimization_barrier((high_across, to_ahead))
    low_behind = plane_shift(add_wide(*piece(1, 0), low_across), 1, 1)
    high_ahead = plane_shift(add_wide(*piece(3, 1), high_across), 1, -1)
    low = (low_behind, low_ahead)
    high = (high_behind, high_ahead)

    def column(at):
        received = low if at < 2 else high
        return add_wide(own[0, at], other[0][at], received[0][at % 2], received[1][at % 2])

    return add_wide(
        column(0),
        plane_shift(column(1), 0, 1),
        plane_shift(column(2), 0, 2),
        plane_shift(column(3), 0, -1),
    )


def columns(x):
    return x[:, :128] + x[:, 128:256] + x[:, 256:384]


def column_specs(units, slice_width, at, which=0):
    return [
        pl.BlockSpec((units, slice_width), lambda s, *t, j=j: (0, t[which][at(s) * 2 + j]))
        for j in range(2)
    ]


def forward_body(rows, width, table, *refs):
    pieces, gate_refs, up_refs, scale_ref = refs[0:8], refs[8:10], refs[10:12], refs[12]
    act_ref, left_ref, slope_ref, lin_ref = refs[13:17]
    gate_acc, up_acc, square_acc, held, sems = refs[17:]
    step = pl.program_id(0)

    def copy(piece, at):
        span = piece.at[:, pl.ds(0, rows + GAIN_ROWS), :]
        return pltpu.make_async_copy(span, held.at[at], sems.at[at])

    @pl.when(step == 0)
    def _():
        for at, piece in enumerate(pieces):
            copy(piece, at).start()
        gate_acc[...] = jnp.zeros_like(gate_acc)
        up_acc[...] = jnp.zeros_like(up_acc)
        square_acc[...] = jnp.zeros_like(square_acc)

    copy(pieces[0], step).wait()
    scaled, squares = [], square_acc[...]
    for j in range(2):
        wide = held[step, j, :rows, :].astype(jnp.float32)
        gain = held[step, j, rows:, :].astype(jnp.float32)[:1, :]
        squares = squares + columns(wide * wide)
        scaled.append((wide * gain).astype(jnp.bfloat16))
    square_acc[...] = squares
    left = jnp.concatenate(scaled, axis=1)
    gate = jnp.concatenate([r[...] for r in gate_refs], axis=0)
    up = jnp.concatenate([r[...] for r in up_refs], axis=0)
    gate_acc[...] += jnp.dot(left, gate, preferred_element_type=jnp.float32)
    up_acc[...] += jnp.dot(left, up, preferred_element_type=jnp.float32)

    @pl.when(step == 7)
    def _():
        total = jnp.sum(square_acc[...], axis=1, keepdims=True)
        scaling = lax.rsqrt(total / width + 1e-05)
        gate_pre = gate_acc[...] * scaling
        up_proj = up_acc[...] * scaling
        sigmoid_gate = jax.nn.sigmoid(gate_pre)
        activated = gate_pre * sigmoid_gate
        act = (activated * up_proj).astype(jnp.bfloat16)
        act_ref[...] = act
        left_ref[...] = (act.astype(jnp.float32) * scale_ref[:, :1]).astype(jnp.bfloat16)
        slope = up_proj * sigmoid_gate * (1.0 + gate_pre * (1.0 - sigmoid_gate))
        scaling = scaling * scale_ref[:, :1]
        slope_ref[...] = slope * scaling
        lin_ref[...] = activated * scaling


def forward(pieces, table, gate_mat, up_mat, row_scale):
    slice_width = pieces[0].shape[2]
    rows = row_scale.shape[0]
    width, units = gate_mat.shape
    row_specs = [
        pl.BlockSpec((slice_width, units), lambda s, t, j=j: (t[s * 2 + j], 0)) for j in range(2)
    ]
    whole = pl.BlockSpec((rows, units), lambda s, t: (0, 0))
    wide = jax.ShapeDtypeStruct((rows, units), jnp.float32)
    narrow = jax.ShapeDtypeStruct((rows, units), jnp.bfloat16)
    return pl.pallas_call(
        functools.partial(forward_body, rows, width),
        out_shape=(narrow, narrow, wide, wide),
        grid_spec=pltpu.PrefetchScalarGridSpec(
            num_scalar_prefetch=1,
            grid=(8,),
            in_specs=[pl.BlockSpec(memory_space=pl.ANY)] * 8
            + row_specs
            + row_specs
            + [pl.BlockSpec((rows, 128), lambda s, t: (0, 0))],
            out_specs=[whole, whole, whole, whole],
            scratch_shapes=[
                pltpu.VMEM((rows, units), jnp.float32),
                pltpu.VMEM((rows, units), jnp.float32),
                pltpu.VMEM((rows, 128), jnp.float32),
                pltpu.VMEM((8, 2, rows + GAIN_ROWS, slice_width), jnp.bfloat16),
                pltpu.SemaphoreType.DMA((8,)),
            ],
        ),
        compiler_params=pltpu.CompilerParams(vmem_limit_bytes=VMEM_LIMIT),
        cost_estimate=pl.CostEstimate(
            flops=4 * rows * width * units, transcendentals=rows * units, bytes_accessed=11 << 20
        ),
        name="forward",
    )(table, *pieces, *([gate_mat] * 2), *([up_mat] * 2), row_scale)


def down_body(table, act_ref, low_ref, high_ref, part_ref):
    for j, ref in enumerate((low_ref, high_ref)):
        part = jnp.dot(act_ref[...], ref[...], preferred_element_type=jnp.float32)
        part_ref[0, j] = part.astype(jnp.bfloat16)


def down(act, table, first, count, down_mat):
    rows, units = act.shape
    slice_width = down_mat.shape[1] // 16

    def at(s):
        return s + 2 * first

    return pl.pallas_call(
        down_body,
        out_shape=jax.ShapeDtypeStruct((count, 4, rows, slice_width), jnp.bfloat16),
        grid_spec=pltpu.PrefetchScalarGridSpec(
            num_scalar_prefetch=1,
            grid=(2 * count,),
            in_specs=[pl.BlockSpec((rows, units), lambda s, t: (0, 0))]
            + column_specs(units, slice_width, at),
            out_specs=pl.BlockSpec((1, 2, rows, slice_width), lambda s, t: (s // 2, s % 2, 0, 0)),
        ),
        compiler_params=pltpu.CompilerParams(vmem_limit_bytes=VMEM_LIMIT),
        cost_estimate=pl.CostEstimate(
            flops=8 * count * rows * units * slice_width,
            transcendentals=0,
            bytes_accessed=count * (2 << 20),
        ),
        name="down",
    )(table, act, down_mat, down_mat)


def part_of(table, numbers):
    return jnp.concatenate([table[2 * number : 2 * number + 2] for number in numbers])


def grads_step(rows, count, refs, grad_acc, held, sems):
    pieces = refs[0 : 2 * count]
    own_refs, other_refs = refs[2 * count : 2 * count + 2], refs[2 * count + 2 : 2 * count + 4]
    step = pl.program_id(0)

    def copy(piece, at):
        span = piece.at[:, pl.ds(rows + GAIN_ROWS, rows), :]
        return pltpu.make_async_copy(span, held.at[at], sems.at[at])

    @pl.when(step == 0)
    def _():
        for at in range(count):
            copy(pieces[at], at).start()
            copy(pieces[at + count], at + count).start()

    dims = (((1,), (1,)), ((), ()))
    copy(pieces[0], step).wait()
    cot = jnp.concatenate([held[step, j] for j in range(2)], axis=1)
    mat = jnp.concatenate([r[...] for r in own_refs], axis=1)
    grad_acc[:rows, :] += lax.dot_general(cot, mat, dims, preferred_element_type=jnp.float32)
    copy(pieces[0], step + count).wait()
    cot = jnp.concatenate([held[step + count, j] for j in range(2)], axis=1)
    mat = jnp.concatenate([r[...] for r in other_refs], axis=1)
    grad_acc[rows:, :] += lax.dot_general(cot, mat, dims, preferred_element_type=jnp.float32)


def grads_early(rows, count, table, other_table, *refs):
    grad_acc, held, sems = refs[-3:]

    @pl.when(pl.program_id(0) == 0)
    def _():
        grad_acc[...] = jnp.zeros_like(grad_acc)

    grads_step(rows, count, refs, grad_acc, held, sems)


def grads_late(rows, count, table, other_table, *refs):
    before, act_o, act_p, slope_o, slope_p, lin_o, lin_p, left_ref, acts_ref = refs[
        2 * count + 4 : 2 * count + 13
    ]
    grad_acc, held, sems = refs[-3:]
    step = pl.program_id(0)

    @pl.when(step == 0)
    def _():
        grad_acc[...] = before[...]

    grads_step(rows, count, refs, grad_acc, held, sems)

    @pl.when(step == count - 1)
    def _():
        units = grad_acc.shape[1]
        grad = grad_acc[...]
        slope = jnp.concatenate([slope_o[...], slope_p[...]], axis=0)
        lin = jnp.concatenate([lin_o[...], lin_p[...]], axis=0)
        left_ref[:units, :] = (grad * slope).T.astype(jnp.bfloat16)
        left_ref[units:, :] = (grad * lin).T.astype(jnp.bfloat16)
        act = jnp.concatenate([act_o[...], act_p[...]], axis=0).astype(jnp.float32)
        acts_ref[...] = act.T.astype(jnp.bfloat16)


def activation_grads(tables, own, other, numbers, down_mat, before=None, saved=None):
    slice_width = own[0].shape[2]
    rows = (own[0].shape[1] - GAIN_ROWS) // 2
    units, width = down_mat.shape
    count = len(numbers)
    whole = pl.BlockSpec((rows, units), lambda s, *t: (0, 0))
    double = pl.BlockSpec((2 * rows, units), lambda s, *t: (0, 0))

    def at(s):
        return s

    in_specs = (
        [pl.BlockSpec(memory_space=pl.ANY)] * (2 * count)
        + column_specs(units, slice_width, at, 0)
        + column_specs(units, slice_width, at, 1)
    )
    operands = [side[number] for side in (own, other) for number in numbers] + [down_mat] * 4
    scratch = [
        pltpu.VMEM((2 * count, 2, rows, slice_width), jnp.bfloat16),
        pltpu.SemaphoreType.DMA((2 * count,)),
    ]
    if saved is None:
        body = functools.partial(grads_early, rows, count)
        out_shape = jax.ShapeDtypeStruct((2 * rows, units), jnp.float32)
        out_specs = double
    else:
        body = functools.partial(grads_late, rows, count)
        out_shape = (
            jax.ShapeDtypeStruct((2 * units, 2 * rows), jnp.bfloat16),
            jax.ShapeDtypeStruct((units, 2 * rows), jnp.bfloat16),
        )
        out_specs = [
            pl.BlockSpec((2 * units, 2 * rows), lambda s, *t: (0, 0)),
            pl.BlockSpec((units, 2 * rows), lambda s, *t: (0, 0)),
        ]
        in_specs = in_specs + [double] + [whole] * 6
        operands += [before, *saved]
        scratch = [pltpu.VMEM((2 * rows, units), jnp.float32)] + scratch
    return pl.pallas_call(
        body,
        out_shape=out_shape,
        grid_spec=pltpu.PrefetchScalarGridSpec(
            num_scalar_prefetch=2,
            grid=(count,),
            in_specs=in_specs,
            out_specs=out_specs,
            scratch_shapes=scratch,
        ),
        compiler_params=pltpu.CompilerParams(vmem_limit_bytes=VMEM_LIMIT),
        cost_estimate=pl.CostEstimate(
            flops=count * rows * width * units // 2,
            transcendentals=0,
            bytes_accessed=count * (7 << 18),
        ),
        name="grads",
    )(*(part_of(table, numbers) for table in tables), *operands)


def score_body(rows, start, steps, table, left_ref, acts_ref, *refs):
    places = score_pieces(start, steps)
    pieces = dict(zip(places, refs[: len(places)], strict=True))
    refs = refs[len(places) :]
    down_refs, gate_refs, up_refs, out_ref = refs[0:2], refs[2:4], refs[4:6], refs[6]
    own_held, other_held, own_sems, other_sems = refs[7:]
    here = pl.program_id(0)

    @pl.when(here == 0)
    def _():
        for at in range(steps):
            i, h = divmod(start + at, 2)
            pltpu.make_async_copy(
                pieces[0, start + at], own_held.at[at], own_sems.at[at]
            ).start()
            for j in range(2):
                source = pieces[1, 2 * (2 * h + j) + i // 2].at[i % 2]
                pltpu.make_async_copy(source, other_held.at[at, j], other_sems.at[at, j]).start()
        out_ref[...] = jnp.zeros_like(out_ref)

    pltpu.make_async_copy(pieces[0, start], own_held.at[here], own_sems.at[here]).wait()
    units = acts_ref.shape[0]
    cots = rows + GAIN_ROWS
    total = out_ref[...]
    for j in range(2):
        source = pieces[0, start].at[j]
        pltpu.make_async_copy(source, other_held.at[here, j], other_sems.at[here, j]).wait()
        gain = own_held[here, j, rows:cots, :].astype(jnp.float32)[:1, :]
        right = jnp.concatenate([own_held[here, j, :rows, :], other_held[here, j, :rows, :]], axis=0)
        grads = jnp.dot(left_ref[...], right, preferred_element_type=jnp.float32)
        gate = jnp.abs(grads[:units, :] * gate_refs[j][...].astype(jnp.float32))
        up = jnp.abs(grads[units:, :] * up_refs[j][...].astype(jnp.float32))
        total = total + columns((gate + up) * jnp.abs(gain))
        right = jnp.concatenate([own_held[here, j, cots:, :], other_held[here, j, cots:, :]], axis=0)
        grads = jnp.dot(acts_ref[...], right, preferred_element_type=jnp.float32)
        total = total + columns(jnp.abs(grads * down_refs[j][...].astype(jnp.float32)))
    out_ref[...] = total


def score_pieces(start, steps):
    places = [(0, start + at) for at in range(steps)]
    for at in range(steps):
        i, h = divmod(start + at, 2)
        for j in range(2):
            place = (1, 2 * (2 * h + j) + i // 2)
            if place not in places:
                places.append(place)
    return places


def score(start, steps, table, lefts, pieces, mats):
    total_rows, slice_width = pieces[0].shape[1:]
    rows = (total_rows - GAIN_ROWS) // 2
    units = lefts[1].shape[0]
    used = [pieces[8 * side + number] for side, number in score_pieces(start, steps)]

    def at(s):
        return s + start

    down_mat, gate_cols, up_cols = mats
    columns_of = column_specs(units, slice_width, at)
    return pl.pallas_call(
        functools.partial(score_body, rows, start, steps),
        out_shape=jax.ShapeDtypeStruct((units, 128), jnp.float32),
        grid_spec=pltpu.PrefetchScalarGridSpec(
            num_scalar_prefetch=1,
            grid=(steps,),
            in_specs=[
                pl.BlockSpec((2 * units, 2 * rows), lambda s, t: (0, 0)),
                pl.BlockSpec((units, 2 * rows), lambda s, t: (0, 0)),
            ]
            + [pl.BlockSpec(memory_space=pl.ANY)] * len(used)
            + columns_of
            + columns_of
            + columns_of,
            out_specs=pl.BlockSpec((units, 128), lambda s, t: (0, 0)),
            scratch_shapes=[
                pltpu.VMEM((steps, 2, total_rows, slice_width), jnp.bfloat16),
                pltpu.VMEM((steps, 2, total_rows, slice_width), jnp.bfloat16),
                pltpu.SemaphoreType.DMA((steps,)),
                pltpu.SemaphoreType.DMA((steps, 2)),
            ],
        ),
        compiler_params=pltpu.CompilerParams(vmem_limit_bytes=VMEM_LIMIT),
        cost_estimate=pl.CostEstimate(
            flops=12 * rows * units * slice_width * 2 * steps,
            transcendentals=0,
            bytes_accessed=steps * (5 << 19),
        ),
        name="score",
    )(
        table,
        *lefts,
        *used,
        *([down_mat] * 2),
        *([gate_cols] * 2),
        *([up_cols] * 2),
    )


def turn_body(gate_ref, up_ref, gate_out, up_out):
    gate_out[...] = gate_ref[...].T
    up_out[...] = up_ref[...].T


def turned(gate_mat, up_mat):
    width, units = gate_mat.shape
    count = 8
    tall = pl.BlockSpec((width // count, units), lambda s: (s, 0))
    flat = pl.BlockSpec((units, width // count), lambda s: (0, s))
    shape = jax.ShapeDtypeStruct((units, width), gate_mat.dtype)
    return pl.pallas_call(
        turn_body,
        out_shape=(shape, shape),
        grid=(count,),
        in_specs=[tall, tall],
        out_specs=[flat, flat],
        compiler_params=pltpu.CompilerParams(vmem_limit_bytes=VMEM_LIMIT),
        cost_estimate=pl.CostEstimate(flops=0, transcendentals=0, bytes_accessed=12 << 20),
        name="turn",
    )(gate_mat, up_mat)


def on_device(hidden, gain, expert_ids, gate_weights, segment_ids, upstream, w_gate, w_up, w_down):
    rows_here, slice_width = hidden.shape
    top_count = expert_ids.shape[1]
    experts = lax.axis_size("tok")
    groups = lax.axis_size("grp")
    capacity = 5 * rows_here // (2 * experts)
    side = math.isqrt(lax.axis_size("tp"))
    place = lax.axis_index("tp")
    row_at, col_at = place // side, place % side
    outer = jnp.arange(side * side, dtype=jnp.int32) // side
    inner = jnp.arange(side * side, dtype=jnp.int32) % side
    first_core = lax.axis_index("grp") == 0
    row_step = jnp.where(first_core, outer, inner)
    col_step = jnp.where(first_core, inner, outer)
    table = (row_at + row_step) % side * side + (col_at + col_step) % side
    other_table = (row_at + col_step) % side * side + (col_at + row_step) % side

    documents = jnp.arange(experts * groups, dtype=jnp.int32)
    doc_onehot = (segment_ids[:, None] == documents[None, :]).astype(jnp.float32)
    counts = jnp.sum(doc_onehot, axis=0)

    onehot = (
        expert_ids.reshape(-1)[:, None] == jnp.arange(experts, dtype=jnp.int32)[None, :]
    ).astype(jnp.int32)
    before = jnp.cumsum(onehot, axis=0) - onehot
    slot_ids = jnp.sum(before * onehot, axis=1).reshape(rows_here, top_count)

    def matches_of(stride):
        targets = expert_ids * stride + slot_ids
        all_slots = jnp.arange(experts * stride, dtype=jnp.int32)
        return all_slots[:, None, None] == targets[None, :, :]

    def to_experts(block, stride):
        block = block.reshape(experts, stride, slice_width)
        return lax.all_to_all(block, "tok", split_axis=0, concat_axis=0, tiled=True)

    stride = 2 * capacity + 8
    at_slot = jnp.arange(experts * stride, dtype=jnp.int32)
    tokens = jnp.concatenate([hidden, upstream], axis=0)
    targets = expert_ids * stride + slot_ids
    targets = jnp.concatenate([targets, targets + capacity], axis=0)
    placing = jnp.any(at_slot[:, None, None] == targets[None, :, :], axis=2).astype(jnp.bfloat16)
    count_lanes = jnp.pad(counts, (0, slice_width - counts.shape[0]))
    count_rows = jnp.where(
        at_slot[:, None] % stride == 2 * capacity, count_lanes[None, :], 0.0
    )
    blocks = jnp.dot(placing, tokens, preferred_element_type=jnp.float32) + count_rows
    came = to_experts(blocks.astype(jnp.bfloat16), stride)
    came_rows = came[:, :capacity].reshape(experts * capacity, slice_width)
    came_cot = came[:, capacity : 2 * capacity].reshape(experts * capacity, slice_width)
    gain_rows = jnp.broadcast_to(gain[None, :], (GAIN_ROWS, slice_width))
    own_pieces = plane_gather(jnp.concatenate([came_rows, gain_rows, came_cot], axis=0))
    other_pieces = [swap_cores(piece) for piece in own_pieces]

    doc_half = jnp.sum(came[:, 2 * capacity, : counts.shape[0]].astype(jnp.float32), axis=0)
    doc_len = doc_half + swap_cores(doc_half)
    tok_len = jnp.sum(doc_onehot * doc_len[None, :], axis=1)
    tok_weight = rows_here / tok_len
    scaled = gate_weights * tok_weight[:, None]
    matches = matches_of(capacity)
    slot_scale = jnp.sum(jnp.where(matches, scaled[None, :, :], 0.0), axis=(1, 2))
    combining = jnp.sum(jnp.where(matches, gate_weights[None, :, :], 0.0), axis=2)
    wide_scale = jnp.broadcast_to(slot_scale[:, None], (experts * capacity, 128))
    scale_own = lax.all_to_all(
        wide_scale.reshape(experts, capacity, 128),
        "tok",
        split_axis=0,
        concat_axis=0,
        tiled=True,
    ).reshape(experts * capacity, 128)
    scale_other = swap_cores(scale_own)

    gate_mat, up_mat, down_mat = w_gate[0], w_up[0], w_down[0]
    gate_cols, up_cols = turned(gate_mat, up_mat)
    tables = (table, other_table)
    sums_grad = activation_grads(tables, own_pieces, other_pieces, EARLY, down_mat)
    act_own, left_own, slope_own, lin_own = forward(own_pieces, table, gate_mat, up_mat, scale_own)
    part_own = down(act_own, table, 0, 4, down_mat)
    act_other, left_other, slope_other, lin_other = forward(
        other_pieces, other_table, gate_mat, up_mat, scale_other
    )
    part_other = {}
    for at in (2, 1, 3, 0):
        part = down(act_other, other_table, at, 1, down_mat)
        part_other[at] = swap_cores(part[0])
    outgoing = plane_scatter(part_own, part_other)

    saved = (left_own, left_other, slope_own, slope_other, lin_own, lin_other)
    lefts = activation_grads(
        tables, own_pieces, other_pieces, LATE, down_mat, sums_grad, saved
    )
    scores = 0.0
    for start, steps in SCORE_STEPS:
        scores = scores + score(
            start,
            steps,
            table,
            lefts,
            own_pieces + other_pieces,
            (down_mat, gate_cols, up_cols),
        )
    importance = jnp.sum(scores, axis=1) / (rows_here * experts * groups)

    returned = to_experts(outgoing, capacity)
    returned = returned.reshape(experts * capacity, slice_width).astype(jnp.float32)
    combined = jnp.dot(
        combining.T, returned, precision=lax.Precision.HIGHEST, preferred_element_type=jnp.float32
    )
    mixed = (hidden.astype(jnp.float32) + combined).astype(jnp.bfloat16)
    return (mixed, importance[None, :])


def solution(mesh):
    placed = (
        P(("tok", "grp"), "tp"),
        P("tp"),
        P(("tok", "grp"), None),
        P(("tok", "grp"), None),
        P(("tok", "grp")),
        P(("tok", "grp"), "tp"),
        P("tok", None, ("tp", "grp")),
        P("tok", None, ("tp", "grp")),
        P("tok", ("tp", "grp"), None),
    )
    return jax.shard_map(
        on_device,
        mesh=mesh,
        in_specs=placed,
        out_specs=(P(("tok", "grp"), "tp"), P("tok", ("tp", "grp"))),
        check_vma=False,
    )
```
